128 devices in a mesh: dp: 8 (over x_lo, z), space: 16 (over y, x_hi, core).
Axes of the slice: x: 4 (x_hi: 2, x_lo: 2; x = x_hi * 2 + x_lo), y: 4, z: 4, core: 2. Of those that a mesh axis runs over, the one named last changes fastest.
Arguments:
- features: bfloat16 [8, 96, 16, 112, 448], P('dp', None, None, 'space'), may hold values from -6 to 6
- conv_weight: bfloat16 [3, 3, 3, 3, 96], replicated, may hold values from -0.125 to 0.125
- out_grad: bfloat16 [8, 16, 256, 384], P('dp', 'space'), may hold values from -6 to 6
- pos_embed: bfloat16 [256, 384], replicated, may hold values from -3 to 3
- patch_weight: bfloat16 [588, 384], replicated, may hold values from -0.25 to 0.25
- norm1: float32 [384], replicated, may hold values from 0.1 to 1.9
- qkv_weight: bfloat16 [384, 1152], replicated, may hold values from -0.3125 to 0.3125
- proj_weight: bfloat16 [384, 384], replicated, may hold values from -0.3125 to 0.3125
- norm2: float32 [384], replicated, may hold values from 0.1 to 1.9
- fc1_weight: bfloat16 [384, 1536], replicated, may hold values from -0.3125 to 0.3125
- fc2_weight: bfloat16 [1536, 384], replicated, may hold values from -0.15625 to 0.15625
Outputs:
- block_out: bfloat16 [8, 16, 256, 384], P('dp', 'space')
- feature_grad: bfloat16 [8, 96, 16, 112, 448], P('dp', None, None, 'space')
- conv_grad: float32 [3, 3, 3, 3, 96], replicated
- qkv_grad: float32 [384, 1152], P('space')
- proj_grad: float32 [384, 384], P('space')
- fc1_grad: float32 [384, 1536], P('space')
- fc2_grad: float32 [1536, 384], P('space')
The draws below stay inside these ranges and needn't reach their ends.
All inputs are finite; a program needn't handle non-finite values.
Results may differ from the reference program's by a relative error of at most 0.025.
Values may be sent and summed in bfloat16 or wider, within the bound.
A program may use at most 192 MiB of HBM per device.

```python
import jax
import jax.numpy as jnp
from jax import lax

D = 384
HEADS = 6
MLP = 1536
CH = 96
FRAMES = 16
ROWS_DEV = 7
COLS = 448
H = 112
PATCHES = 256
CLIPS = 8
N_DP = 8
N_SPACE = 16


def block_scale(rng, dims, cuts, least, top_value):
    level, own = 1.0, jax.random.fold_in(rng, 6)
    for position, blocks in cuts:
        heights = jnp.exp(jax.random.uniform(jax.random.fold_in(own, position), (blocks,), jnp.float32, least / len(cuts), top_value / len(cuts)))
        level = level * jnp.repeat(heights, dims[position] // blocks).reshape([-1 if axis == position else 1 for axis in range(len(dims))])
    return level


def normal_values(rng, shape, spread, reach, shards=(), held_as=jnp.bfloat16):
    values = spread * jax.random.normal(rng, shape, jnp.float32)
    if shards:
        values = values * block_scale(rng, shape, shards, -0.22, 0.18)
    return jnp.clip(values, -reach, reach).astype(held_as)


def setup_inputs(seed: int = 0) -> dict:
    splits = jax.random.split(jax.random.key(seed), 12)
    features = normal_values(splits[0], (CLIPS, CH, FRAMES, H, COLS), 1.0, 6.0, ((0, 8), (3, 16)))
    conv_weight = normal_values(splits[1], (3, 3, 3, 3, CH), (27 * CH) ** -0.5, 0.125)
    out_grad = normal_values(splits[2], (CLIPS, FRAMES, PATCHES, D), 1.0, 6.0, ((0, 8), (1, 16)))
    pos_embed = normal_values(splits[3], (PATCHES, D), 0.5, 3.0)
    patch_weight = normal_values(splits[4], (588, D), 588 ** -0.5, 0.25)
    norm1 = jnp.clip(1.0 + 0.18 * jax.random.normal(splits[5], (D,), jnp.float32), 0.1, 1.9)
    qkv_weight = normal_values(splits[6], (D, 3 * D), D ** -0.5, 0.3125)
    proj_weight = normal_values(splits[7], (D, D), D ** -0.5, 0.3125)
    norm2 = jnp.clip(1.0 + 0.18 * jax.random.normal(splits[8], (D,), jnp.float32), 0.1, 1.9)
    fc1_weight = normal_values(splits[9], (D, MLP), D ** -0.5, 0.3125)
    fc2_weight = normal_values(splits[10], (MLP, D), MLP ** -0.5, 0.15625)
    return dict(features=features, conv_weight=conv_weight, out_grad=out_grad, pos_embed=pos_embed, patch_weight=patch_weight, norm1=norm1, qkv_weight=qkv_weight, proj_weight=proj_weight, norm2=norm2, fc1_weight=fc1_weight, fc2_weight=fc2_weight)


def layer_norm(values, gain_vec):
    average = lax.optimization_barrier(jnp.mean(values, axis=-1, keepdims=True))
    centered = values - average
    variance = lax.optimization_barrier(jnp.mean(centered * centered, axis=-1, keepdims=True))
    return centered * lax.rsqrt(variance + 1e-06) * gain_vec

def discriminator(pixels, pos_embed, patch_weight, norm1, qkv_weight, proj_weight, norm2, fc1_weight, fc2_weight):
    channels, height, width = pixels.shape
    patch_rows = height // 14
    patch_cols = width // 14
    count = patch_rows * patch_cols
    patches = pixels.reshape(channels, patch_rows, 14, patch_cols, 14).transpose(1, 3, 0, 2, 4).reshape(count, channels * 196)
    embedded = jnp.dot(patches, patch_weight, preferred_element_type=jnp.float32) + pos_embed.astype(jnp.float32)
    model_width = embedded.shape[1]
    normed = layer_norm(embedded, norm1).astype(jnp.bfloat16)
    packed = jnp.dot(normed, qkv_weight, preferred_element_type=jnp.float32).astype(jnp.bfloat16)
    packed = packed.reshape(count, 3, HEADS, model_width // HEADS)
    queries = packed[:, 0]
    keys_in = packed[:, 1]
    values_in = packed[:, 2]
    head_size = model_width // HEADS
    scores = jnp.einsum('qhd,khd->hqk', queries, keys_in, preferred_element_type=jnp.float32) * (1.0 / float(head_size) ** 0.5)
    probs = jax.nn.softmax(scores, axis=-1).astype(jnp.bfloat16)
    attended = jnp.einsum('hqk,khd->qhd', probs, values_in, preferred_element_type=jnp.float32)
    attended = attended.astype(jnp.bfloat16).reshape(count, model_width)
    residual = embedded + jnp.dot(attended, proj_weight, preferred_element_type=jnp.float32)
    normed_two = layer_norm(residual, norm2).astype(jnp.bfloat16)
    hidden = jax.nn.gelu(jnp.dot(normed_two, fc1_weight, preferred_element_type=jnp.float32), approximate=False).astype(jnp.bfloat16)
    return residual + jnp.dot(hidden, fc2_weight, preferred_element_type=jnp.float32)

def frame_steps(frames, cotangents, params):
    pos_embed, patch_weight, norm1, qkv_weight, proj_weight, norm2, fc1_weight, fc2_weight = params

    def one_frame(pixels, cotangent):

        def forward(pix, qkv_w, proj_w, fc1_w, fc2_w):
            return discriminator(pix, pos_embed, patch_weight, norm1, qkv_w, proj_w, norm2, fc1_w, fc2_w)
        result, pullback = jax.vjp(forward, pixels, qkv_weight, proj_weight, fc1_weight, fc2_weight)
        cotans = pullback(cotangent.astype(jnp.float32))
        return (result.astype(jnp.bfloat16), cotans[0], tuple((item.astype(jnp.float32) for item in cotans[1:])))
    block_out, pixel_grads, weight_grads = jax.vmap(one_frame, in_axes=(1, 0), out_axes=(0, 1, 0))(frames, cotangents)
    return (block_out, pixel_grads, tuple((lax.optimization_barrier(jnp.sum(item, axis=0)) for item in weight_grads)))

def project_taps(feature_tile, tap_matrix):
    return lax.dot_general(tap_matrix, feature_tile, (((1,), (0,)), ((), ())), preferred_element_type=jnp.float32)

def time_parts(tap_values):
    grouped = tap_values.reshape((3, 3, 9) + tap_values.shape[1:])
    frame_count = tap_values.shape[1]
    parts = []
    for row_tap in range(3):
        total = None
        for time_tap in range(3):
            piece = grouped[time_tap, row_tap]
            lag = 2 - time_tap
            if lag > 0:
                piece = jnp.pad(piece[:, :frame_count - lag], ((0, 0), (lag, 0), (0, 0), (0, 0)))
            total = piece if total is None else total + piece
        parts.append(total)
    return parts

def column_sum(planes):
    width = planes.shape[-1]
    padded = jnp.pad(planes, ((0, 0), (0, 0), (0, 0), (1, 1)))
    return padded[0:3, :, :, 0:width] + padded[3:6, :, :, 1:1 + width] + padded[6:9, :, :, 2:2 + width]

def gather_taps(padded_grad, frame_count, row_count, col_count):
    shifted = [padded_grad[:, :, :, 2 - col_tap:2 - col_tap + col_count] for col_tap in range(3)]
    pieces = []
    for time_tap in range(3):
        for row_tap in range(3):
            for col_tap in range(3):
                pieces.append(shifted[col_tap][:, 2 - time_tap:2 - time_tap + frame_count, 2 - row_tap:2 - row_tap + row_count])
    return jnp.stack(pieces, axis=0).reshape(-1, frame_count * row_count * col_count)

def conv_backward(stacked, feature_tile, tap_matrix):
    channels = feature_tile.shape[0]
    flat = feature_tile.reshape(channels, -1)
    feature_grad = lax.dot_general(tap_matrix, stacked, (((0,), (0,)), ((), ())), preferred_element_type=jnp.float32)
    feature_grad = feature_grad.reshape(feature_tile.shape).astype(jnp.bfloat16)
    conv_part = lax.dot_general(stacked, flat, (((1,), (1,)), ((), ())), preferred_element_type=jnp.float32)
    return (feature_grad, conv_part)

def reference(features, conv_weight, out_grad, pos_embed, patch_weight, norm1, qkv_weight, proj_weight, norm2, fc1_weight, fc2_weight):
    params = (pos_embed, patch_weight, norm1, qkv_weight, proj_weight, norm2, fc1_weight, fc2_weight)
    tap_matrix = conv_weight.reshape(-1, CH)
    height = ROWS_DEV * N_SPACE
    blocks = []
    feature_grads = []
    conv_total = jnp.zeros(tap_matrix.shape, jnp.float32)
    totals = (jnp.zeros(qkv_weight.shape, jnp.float32), jnp.zeros(proj_weight.shape, jnp.float32), jnp.zeros(fc1_weight.shape, jnp.float32), jnp.zeros(fc2_weight.shape, jnp.float32))
    for clip in range(N_DP):
        feature_clip = features[clip]
        parts = time_parts(project_taps(feature_clip, tap_matrix))
        planes = None
        for row_tap in range(3):
            piece = jnp.pad(parts[row_tap], ((0, 0), (0, 0), (1, 1), (0, 0)))[:, :, row_tap:row_tap + height]
            planes = piece if planes is None else planes + piece
        pixels = column_sum(planes).astype(jnp.bfloat16)
        block_out, pixel_grads, weight_grads = frame_steps(pixels, out_grad[clip], params)
        padded_grad = jnp.pad(pixel_grads, ((0, 0), (0, 2), (1, 1), (1, 1)))
        stacked = gather_taps(padded_grad, FRAMES, height, COLS)
        feature_grad, conv_part = conv_backward(stacked, feature_clip, tap_matrix)
        blocks.append(block_out)
        feature_grads.append(feature_grad)
        conv_total = conv_total + conv_part
        totals = tuple((total + item for total, item in zip(totals, weight_grads)))
    return (jnp.stack(blocks, axis=0), jnp.stack(feature_grads, axis=0), conv_total.reshape(conv_weight.shape), totals[0], totals[1], totals[2], totals[3])
```

```python
import functools

import jax
import jax.numpy as jnp
from jax import lax
from jax.experimental import pallas as pl
from jax.experimental.pallas import tpu as pltpu
from jax.sharding import PartitionSpec as P

HEADS = 6
BF = jnp.bfloat16
F32 = jnp.float32
NN = (((1,), (0,)), ((), ()))
NT = (((1,), (1,)), ((), ()))
TN = (((0,), (0,)), ((), ()))


def dot(a, b, dims=NN):
    return lax.dot_general(a, b, dims, preferred_element_type=F32)


def iota(shape, dim):
    return lax.broadcasted_iota(jnp.int32, shape, dim)


def one_hot(cond):
    return jnp.where(cond, 1.0, 0.0).astype(BF)


def group_source(group):
    return (2 - group // 9) * 9 + group % 9


def band(w81):
    spread = one_hot(iota((96, 1536), 1) // 16 == iota((96, 1536), 0))
    row = iota((432, 81), 0)
    source = group_source(row // 16)
    lag = iota((432, 1536), 1) % 16 - iota((432, 1536), 0) % 16 + 2
    total = None
    for a in range(3):
        picked = dot(one_hot(iota((432, 81), 1) == source + 27 * a), w81).astype(BF)
        piece = jnp.where(lag == a, dot(picked, spread), 0.0)
        total = piece if total is None else total + piece
    return total.astype(BF)


def band_transposed(w81):
    spread = one_hot(iota((1536, 96), 0) // 16 == iota((1536, 96), 1))
    source = group_source(iota((81, 432), 1) // 16)
    lag = iota((1536, 432), 0) % 16 - iota((1536, 432), 1) % 16 + 2
    total = None
    for a in range(3):
        picked = dot(w81, one_hot(iota((81, 432), 0) == source + 27 * a), TN).astype(BF)
        piece = jnp.where(lag == a, dot(spread, picked), 0.0)
        total = piece if total is None else total + piece
    return total.astype(BF)


def conv_forward_kernel(w_ref, x_ref, out_ref, band_ref, acc_ref, rows_ref):
    step = pl.program_id(0)

    @pl.when(step == 0)
    def _():
        band_ref[...] = band(w_ref[...])
        acc_ref[...] = jnp.zeros_like(acc_ref)
        rows_ref[...] = jnp.zeros_like(rows_ref)

    x = x_ref[:, 0].reshape(1536, 448)
    at = pl.ds(pl.multiple_of(step * 144, 16), 432)
    acc_ref[at, :448] += dot(band_ref[...], x)

    @pl.when(step == 6)
    def _():
        for row in range(9):
            taps = acc_ref[row * 144 : (row + 1) * 144, :]
            out = pltpu.roll(taps[0:48], 1, 1) + taps[48:96] + pltpu.roll(taps[96:144], 511, 1)
            for o in range(3):
                for t in range(4):
                    rows_ref[t, pl.ds(o * 9 + row, 16, stride=32), :] = out[
                        o * 16 : (o + 1) * 16, t * 128 : t * 128 + 128
                    ]
        for t in range(3):
            out_ref[:, t * 128 : t * 128 + 128] = rows_ref[t].astype(BF)
        out_ref[:, 384:448] = rows_ref[3, :, :64].astype(BF)


def conv_forward(features, w81):
    return pl.pallas_call(
        conv_forward_kernel,
        grid=(7,),
        out_shape=jax.ShapeDtypeStruct((512, 448), BF),
        in_specs=[
            pl.BlockSpec((81, 96), lambda h: (0, 0)),
            pl.BlockSpec((96, 1, 16, 448), lambda h: (0, h, 0, 0)),
        ],
        out_specs=pl.BlockSpec((512, 448), lambda h: (0, 0)),
        scratch_shapes=[
            pltpu.VMEM((432, 1536), BF),
            pltpu.VMEM((1296, 512), F32),
            pltpu.VMEM((4, 512, 128), F32),
        ],
        name="conv_forward",
    )(w81, features)


def conv_backward_kernel(w_ref, v_ref, x_ref, fg_ref, conv_ref, band_ref, pg_ref, rows_ref, g_ref):
    step = pl.program_id(0)

    @pl.when(step == 0)
    def _():
        band_ref[...] = band_transposed(w_ref[...])
        for t in range(3):
            rows_ref[t] = v_ref[:, t * 128 : t * 128 + 128].astype(F32)
        rows_ref[3] = jnp.zeros((512, 128), F32)
        rows_ref[3, :, :64] = v_ref[:, 384:448].astype(F32)
        for row in range(9):
            for o in range(3):
                v = jnp.concatenate(
                    [rows_ref[t, pl.ds(o * 9 + row, 16, stride=32), :] for t in range(4)], axis=1
                )
                for e in range(3):
                    moved = v if e == 1 else pltpu.roll(v, 511 if e == 0 else 1, 1)
                    at = (row * 9 + e * 3 + o) * 16
                    pg_ref[at : at + 16, :] = moved.astype(BF)
        g_ref[...] = jnp.zeros_like(g_ref)

    x = x_ref[:, 0].reshape(1536, 448)
    pg = pg_ref[pl.ds(pl.multiple_of(step * 144, 16), 432), :448]
    fg_ref[:, 0] = dot(band_ref[...], pg).astype(BF).reshape(96, 16, 448)
    g_ref[...] += dot(pg, x, NT)

    @pl.when(step == 6)
    def _():
        spread = one_hot(iota((1536, 96), 0) // 16 == iota((1536, 96), 1))
        lag = iota((16, 1536), 1) % 16 - iota((16, 1536), 0) + 2
        for a in range(3):
            keep = lag == a
            sums = [
                jnp.sum(jnp.where(keep, g_ref[g * 16 : (g + 1) * 16, :], 0.0), axis=0, keepdims=True)
                for g in range(27)
            ]
            sums = [sums[(2 - b) * 9 + eo] for b in range(3) for eo in range(9)]
            total = jnp.concatenate(sums, axis=0)
            high = total.astype(BF)
            rest = total - high.astype(F32)
            middle = rest.astype(BF)
            conv_ref[a * 27 : (a + 1) * 27, :] = dot(high, spread) + dot(middle, spread)


def conv_backward(features, w81, grad_rows):
    return pl.pallas_call(
        conv_backward_kernel,
        grid=(7,),
        out_shape=(
            jax.ShapeDtypeStruct((96, 7, 16, 448), BF),
            jax.ShapeDtypeStruct((81, 96), F32),
        ),
        in_specs=[
            pl.BlockSpec((81, 96), lambda h: (0, 0)),
            pl.BlockSpec((512, 448), lambda h: (0, 0)),
            pl.BlockSpec((96, 1, 16, 448), lambda h: (0, h, 0, 0)),
        ],
        out_specs=(
            pl.BlockSpec((96, 1, 16, 448), lambda h: (0, h, 0, 0)),
            pl.BlockSpec((81, 96), lambda h: (0, 0)),
        ),
        scratch_shapes=[
            pltpu.VMEM((1536, 432), BF),
            pltpu.VMEM((1296, 512), BF),
            pltpu.VMEM((4, 512, 128), F32),
            pltpu.VMEM((432, 1536), F32),
        ],
        name="conv_backward",
    )(w81, grad_rows, features)


def patch_matrix(patch_weight):
    row = iota((896, 588), 0)
    tile_row = row % 32
    colour, height = tile_row // 9, tile_row % 9
    piece = row // 32
    half, column = piece // 14, piece % 14
    line = (7 * half + height + 13) % 14
    source = colour * 196 + line * 14 + column
    return dot(one_hot((iota((896, 588), 1) == source) & (tile_row < 27)), patch_weight).astype(BF)


def norm_forward(values, gain):
    centered = values - jnp.mean(values, axis=-1, keepdims=True)
    scale = lax.rsqrt(jnp.mean(centered * centered, axis=-1, keepdims=True) + 1e-06)
    unit = centered * scale
    return unit, scale, (unit * gain).astype(BF)


def norm_backward(unit, scale, gain, grad):
    grad = grad * gain
    return scale * (
        grad
        - jnp.mean(grad, axis=-1, keepdims=True)
        - unit * jnp.mean(grad * unit, axis=-1, keepdims=True)
    )


def frame_kernel(
    z_ref, g_ref, pos_ref, pw_ref, n1_ref, wqkv_ref, wproj_ref, n2_ref, w1_ref, w2_ref,
    out_ref, dz_ref, dqkv_ref, dproj_ref, d1_ref, d2_ref,
    wp_ref, a_ref, r_ref, pk_ref, dpk_ref, prob_ref,
):
    wp_ref[...] = patch_matrix(pw_ref[...])
    z = z_ref[...].astype(F32)
    place = iota((512, 448), 0)
    tile, tile_row = place // 32, place % 32
    height = tile_row % 9
    used = tile_row < 27
    above = pltpu.roll(z, 25, 0)
    below = pltpu.roll(z, 487, 0)
    z = z + jnp.where((height == 1) & (tile > 0), above, 0.0)
    z = z + jnp.where((height == 7) & (tile < 15), below, 0.0)
    z = jnp.where(used & (height > 0) & (height < 8), z, 0.0).astype(BF)
    pick = iota((448, 448), 0)
    permute = one_hot(iota((448, 448), 1) == (pick % 32) * 14 + pick // 32)
    turned = dot(permute, z, NT)
    for tile_at in range(16):
        for column in range(14):
            at = ((tile_at % 2) * 14 + column) * 32
            a_ref[tile_at // 2 * 32 : tile_at // 2 * 32 + 32, at : at + 32] = turned[
                column * 32 : column * 32 + 32, tile_at * 32 : tile_at * 32 + 32
            ]
    embedded = dot(a_ref[...].astype(BF), wp_ref[...]) + pos_ref[...].astype(F32)
    gain1, gain2 = n1_ref[...], n2_ref[...]
    unit1, scale1, normed = norm_forward(embedded, gain1)
    pk_ref[...] = dot(normed, wqkv_ref[...]).astype(BF)
    left = iota((256, 128), 1) < 64
    zero = jnp.zeros((256, 128), BF)
    attended = []
    for pair in range(3):
        q = pk_ref[:, pair * 128 : pair * 128 + 128]
        k = pk_ref[:, 384 + pair * 128 : 384 + pair * 128 + 128]
        v = pk_ref[:, 768 + pair * 128 : 768 + pair * 128 + 128]
        both = []
        for side in range(2):
            mine = left if side == 0 else ~left
            s = dot(jnp.where(mine, q, zero), k, NT) * 0.125
            s = jnp.exp(s - jnp.max(s, axis=-1, keepdims=True))
            s = s / jnp.sum(s, axis=-1, keepdims=True)
            prob_ref[pair * 2 + side] = s
            both.append(dot(s.astype(BF), v))
        attended.append(jnp.where(left, both[0], both[1]).astype(BF))
    attended = jnp.concatenate(attended, axis=1)
    residual = embedded + dot(attended, wproj_ref[...])
    unit2, scale2, normed2 = norm_forward(residual, gain2)
    g = g_ref[...]
    out = residual
    dnormed2 = jnp.zeros((256, 384), F32)
    for part in range(3):
        cols = slice(part * 512, part * 512 + 512)
        pre = dot(normed2, w1_ref[:, cols])
        cdf = 0.5 + 0.5 * lax.erf(pre * 0.7071067811865476)
        hidden = (pre * cdf).astype(BF)
        out = out + dot(hidden, w2_ref[cols, :])
        d2_ref[cols, :] = dot(hidden, g, TN).astype(BF)
        dhidden = dot(g, w2_ref[cols, :], NT).astype(BF).astype(F32)
        slope = cdf + pre * (0.3989422804014327 * jnp.exp(-0.5 * pre * pre))
        dpre = (dhidden * slope).astype(BF)
        d1_ref[:, cols] = dot(normed2, dpre, TN).astype(BF)
        dnormed2 = dnormed2 + dot(dpre, w1_ref[:, cols], NT)
    out_ref[...] = out.astype(BF)
    dnormed2 = dnormed2.astype(BF).astype(F32)
    dres = g.astype(F32) + norm_backward(unit2, scale2, gain2, dnormed2)
    dres_bf = dres.astype(BF)
    dproj_ref[...] = dot(attended, dres_bf, TN).astype(BF)
    datt = dot(dres_bf, wproj_ref[...], NT).astype(BF)
    for pair in range(3):
        q = pk_ref[:, pair * 128 : pair * 128 + 128]
        k = pk_ref[:, 384 + pair * 128 : 384 + pair * 128 + 128]
        v = pk_ref[:, 768 + pair * 128 : 768 + pair * 128 + 128]
        da = datt[:, pair * 128 : pair * 128 + 128]
        dq, dk, dv = [], [], []
        for side in range(2):
            mine = left if side == 0 else ~left
            p = prob_ref[pair * 2 + side]
            dp = dot(jnp.where(mine, da, zero), v, NT).astype(BF).astype(F32)
            dv.append(dot(p.astype(BF), da, TN))
            ds = p * (dp - jnp.sum(dp * p, axis=-1, keepdims=True)) * 0.125
            ds = ds.astype(BF)
            dq.append(dot(ds, k))
            dk.append(dot(ds, q, TN))
        dpk_ref[:, pair * 128 : pair * 128 + 128] = jnp.where(left, dq[0], dq[1]).astype(BF)
        dpk_ref[:, 384 + pair * 128 : 384 + pair * 128 + 128] = jnp.where(left, dk[0], dk[1]).astype(BF)
        dpk_ref[:, 768 + pair * 128 : 768 + pair * 128 + 128] = jnp.where(left, dv[0], dv[1]).astype(BF)
    dpk = dpk_ref[...]
    dqkv_ref[...] = dot(normed, dpk, TN).astype(BF)
    dnormed = dot(dpk, wqkv_ref[...], NT).astype(BF).astype(F32)
    demb = dres + norm_backward(unit1, scale1, gain1, dnormed)
    a_ref[...] = dot(demb.astype(BF), wp_ref[...], NT)
    for tile_at in range(16):
        for column in range(14):
            at = ((tile_at % 2) * 14 + column) * 32
            r_ref[column * 32 : column * 32 + 32, tile_at * 32 : tile_at * 32 + 32] = a_ref[
                tile_at // 2 * 32 : tile_at // 2 * 32 + 32, at : at + 32
            ]
    dz = dot(r_ref[...].astype(BF), permute, TN)
    odd = tile % 2 == 1
    nothing = jnp.zeros((64, 448), F32)
    above = jnp.concatenate([nothing, dz[:448]], axis=0)
    below = jnp.concatenate([dz[64:], nothing], axis=0)
    dz = jnp.where((height == 0) & ~odd, above, dz)
    dz = jnp.where((height == 8) & odd, below, dz)
    dz_ref[...] = dz.astype(BF)


def frame_step(z, g, pos, pw, n1, wqkv, wproj, n2, w1, w2):
    return pl.pallas_call(
        frame_kernel,
        out_shape=(
            jax.ShapeDtypeStruct((256, 384), BF),
            jax.ShapeDtypeStruct((512, 448), BF),
            jax.ShapeDtypeStruct((384, 1152), BF),
            jax.ShapeDtypeStruct((384, 384), BF),
            jax.ShapeDtypeStruct((384, 1536), BF),
            jax.ShapeDtypeStruct((1536, 384), BF),
        ),
        scratch_shapes=[
            pltpu.VMEM((896, 384), BF),
            pltpu.VMEM((256, 896), F32),
            pltpu.VMEM((448, 512), F32),
            pltpu.VMEM((256, 1152), BF),
            pltpu.VMEM((256, 1152), BF),
            pltpu.VMEM((6, 256, 256), F32),
        ],
        name="frame_step",
    )(z, g, pos, pw, n1, wqkv, wproj, n2, w1, w2)


def in_blocks(x, length):
    return x.reshape(length, x.shape[0] // length, *x.shape[1:])


def one_scatter(arrays, axis):
    length = lax.axis_size(axis)
    blocks = [in_blocks(a, length) for a in arrays]
    lines = jnp.concatenate([b.reshape(length, -1, 128) for b in blocks], axis=1).reshape(-1, 128)
    mine = lax.psum_scatter(lines, axis, tiled=True)
    return mine, blocks


def from_everyone(x, axis):
    copies = jnp.broadcast_to(x, (lax.axis_size(axis), *x.shape))
    return lax.all_to_all(copies, axis, split_axis=0, concat_axis=0, tiled=True)


def shards(
    features, conv_weight, out_grad, pos_embed, patch_weight, norm1, qkv_weight, proj_weight,
    norm2, fc1_weight, fc2_weight,
):
    tile = features[0].transpose(0, 2, 1, 3)
    w81 = conv_weight.reshape(81, 96)
    rows = conv_forward(tile, w81).reshape(16, 32, 448)
    rows = lax.all_to_all(rows, "space", split_axis=0, concat_axis=0, tiled=True)
    block_out, grad_rows, dqkv, dproj, d1, d2 = frame_step(
        rows.reshape(512, 448), out_grad[0, 0], pos_embed, patch_weight, norm1[None],
        qkv_weight, proj_weight, norm2[None], fc1_weight, fc2_weight,
    )
    grad_rows = lax.all_to_all(
        grad_rows.reshape(16, 32, 448), "space", split_axis=0, concat_axis=0, tiled=True
    )
    feature_grad, conv_part = conv_backward(tile, w81, grad_rows.reshape(512, 448))
    mine, blocks = one_scatter((dqkv, dproj, d1, d2), "space")
    conv_space = from_everyone(conv_part, "space").sum(axis=0)
    total = from_everyone(mine, "dp").astype(F32).sum(axis=0)
    conv_total = from_everyone(conv_space.astype(BF), "dp").astype(F32).sum(axis=0)
    shares, at = [], 0
    for b in blocks:
        part = b[0]
        lines = part.size // 128
        shares.append(total[at : at + lines].reshape(part.shape))
        at += lines
    return (
        block_out[None, None],
        feature_grad.transpose(0, 2, 1, 3)[None],
        conv_total.reshape(conv_weight.shape),
        *shares,
    )


def solution(mesh):
    placed = (
        P("dp", None, None, "space", None),
        P(),
        P("dp", "space", None, None),
        *([P()] * 8),
    )
    return jax.shard_map(
        shards,
        mesh=mesh,
        in_specs=placed,
        out_specs=(
            P("dp", "space", None, None),
            P("dp", None, None, "space", None),
            P(),
            *([P("space", None)] * 4),
        ),
        check_vma=False,
    )
```

```python
import functools

import jax
import jax.numpy as jnp
from jax import lax
from jax.experimental import pallas as pl
from jax.experimental.pallas import tpu as pltpu
from jax.sharding import PartitionSpec as P

HEADS = 6
BF = jnp.bfloat16
F32 = jnp.float32
NN = (((1,), (0,)), ((), ()))
NT = (((1,), (1,)), ((), ()))
TN = (((0,), (0,)), ((), ()))


def dot(a, b, dims=NN):
    return lax.dot_general(a, b, dims, preferred_element_type=F32)


def iota(shape, dim):
    return lax.broadcasted_iota(jnp.int32, shape, dim)


def one_hot(cond):
    return jnp.where(cond, 1.0, 0.0).astype(BF)


def group_source(group):
    return (2 - group // 9) * 9 + group % 9


def band(w81):
    spread = one_hot(iota((96, 1536), 1) // 16 == iota((96, 1536), 0))
    row = iota((432, 81), 0)
    source = group_source(row // 16)
    lag = iota((432, 1536), 1) % 16 - iota((432, 1536), 0) % 16 + 2
    total = None
    for a in range(3):
        picked = dot(one_hot(iota((432, 81), 1) == source + 27 * a), w81).astype(BF)
        piece = jnp.where(lag == a, dot(picked, spread), 0.0)
        total = piece if total is None else total + piece
    return total.astype(BF)


def band_transposed(w81):
    spread = one_hot(iota((1536, 96), 0) // 16 == iota((1536, 96), 1))
    source = group_source(iota((81, 432), 1) // 16)
    lag = iota((1536, 432), 0) % 16 - iota((1536, 432), 1) % 16 + 2
    total = None
    for a in range(3):
        picked = dot(w81, one_hot(iota((81, 432), 0) == source + 27 * a), TN).astype(BF)
        piece = jnp.where(lag == a, dot(spread, picked), 0.0)
        total = piece if total is None else total + piece
    return total.astype(BF)


def conv_forward_kernel(w_ref, x_ref, out_ref, band_ref, acc_ref, rows_ref):
    step = pl.program_id(0)

    @pl.when(step == 0)
    def _():
        band_ref[...] = band(w_ref[...])
        acc_ref[...] = jnp.zeros_like(acc_ref)
        rows_ref[...] = jnp.zeros_like(rows_ref)

    x = x_ref[:, 0].reshape(1536, 448)
    at = pl.ds(pl.multiple_of(step * 144, 16), 432)
    acc_ref[at, :448] += dot(band_ref[...], x)

    @pl.when(step == 6)
    def _():
        for row in range(9):
            taps = acc_ref[row * 144 : (row + 1) * 144, :]
            out = pltpu.roll(taps[0:48], 1, 1) + taps[48:96] + pltpu.roll(taps[96:144], 511, 1)
            for o in range(3):
                for t in range(4):
                    rows_ref[t, pl.ds(o * 9 + row, 16, stride=32), :] = out[
                        o * 16 : (o + 1) * 16, t * 128 : t * 128 + 128
                    ]
        for t in range(3):
            out_ref[:, t * 128 : t * 128 + 128] = rows_ref[t].astype(BF)
        out_ref[:, 384:448] = rows_ref[3, :, :64].astype(BF)


def conv_forward(features, w81):
    return pl.pallas_call(
        conv_forward_kernel,
        grid=(7,),
        out_shape=jax.ShapeDtypeStruct((512, 448), BF),
        in_specs=[
            pl.BlockSpec((81, 96), lambda h: (0, 0)),
            pl.BlockSpec((96, 1, 16, 448), lambda h: (0, h, 0, 0)),
        ],
        out_specs=pl.BlockSpec((512, 448), lambda h: (0, 0)),
        scratch_shapes=[
            pltpu.VMEM((432, 1536), BF),
            pltpu.VMEM((1296, 512), F32),
            pltpu.VMEM((4, 512, 128), F32),
        ],
        name="conv_forward",
    )(w81, features)


def conv_backward_kernel(
    w_ref, v_ref, sums_ref, x_ref,
    fg_ref, conv_ref, qkv_ref, proj_ref, fc1_ref, fc2_ref,
    band_ref, pg_ref, rows_ref, g_ref,
):
    step = pl.program_id(0)

    @pl.when(step == 1)
    def _():
        qkv_ref[...] = sums_ref[0].astype(F32)
        proj_ref[...] = sums_ref[1, :, :384].astype(F32)
        fc1_ref[:, :768] = sums_ref[1, :, 384:].astype(F32)
        fc1_ref[:, 768:] = sums_ref[2, :, :768].astype(F32)
        fc2_ref[0:24] = sums_ref[2, :, 768:].astype(F32)
        for quarter in range(3):
            at = quarter * 24 + 24
            fc2_ref[at : at + 24] = sums_ref[3, :, quarter * 384 : quarter * 384 + 384].astype(F32)

    @pl.when(step == 0)
    def _():
        band_ref[...] = band_transposed(w_ref[...])
        for t in range(3):
            rows_ref[t] = v_ref[:, t * 128 : t * 128 + 128].astype(F32)
        rows_ref[3] = jnp.zeros((512, 128), F32)
        rows_ref[3, :, :64] = v_ref[:, 384:448].astype(F32)
        for row in range(9):
            for o in range(3):
                v = jnp.concatenate(
                    [rows_ref[t, pl.ds(o * 9 + row, 16, stride=32), :] for t in range(4)], axis=1
                )
                for e in range(3):
                    moved = v if e == 1 else pltpu.roll(v, 511 if e == 0 else 1, 1)
                    at = (row * 9 + e * 3 + o) * 16
                    pg_ref[at : at + 16, :] = moved.astype(BF)
        g_ref[...] = jnp.zeros_like(g_ref)
        conv_ref[...] = jnp.zeros_like(conv_ref)

    x = x_ref[:, 0].reshape(1536, 448)
    pg = pg_ref[pl.ds(pl.multiple_of(step * 144, 16), 432), :448]
    fg_ref[:, 0] = dot(band_ref[...], pg).astype(BF).reshape(96, 16, 448)
    g_ref[...] += dot(pg, x, NT)

    @pl.when(step == 6)
    def _():
        spread = one_hot(iota((1536, 96), 0) // 16 == iota((1536, 96), 1))
        lag = iota((16, 1536), 1) % 16 - iota((16, 1536), 0) + 2
        for a in range(3):
            keep = lag == a
            sums = [
                jnp.sum(jnp.where(keep, g_ref[g * 16 : (g + 1) * 16, :], 0.0), axis=0, keepdims=True)
                for g in range(27)
            ]
            sums = [sums[(2 - b) * 9 + eo] for b in range(3) for eo in range(9)]
            total = jnp.concatenate(sums, axis=0)
            high = total.astype(BF)
            rest = total - high.astype(F32)
            middle = rest.astype(BF)
            conv_ref[a * 27 : (a + 1) * 27, :96] = dot(high, spread) + dot(middle, spread)


def conv_backward(features, w81, grad_rows, sums):
    whole = lambda *shape: pl.BlockSpec(shape, lambda h: (0,) * len(shape))
    return pl.pallas_call(
        conv_backward_kernel,
        grid=(7,),
        out_shape=(
            jax.ShapeDtypeStruct((96, 7, 16, 448), BF),
            jax.ShapeDtypeStruct((128, 128), F32),
            jax.ShapeDtypeStruct((24, 1152), F32),
            jax.ShapeDtypeStruct((24, 384), F32),
            jax.ShapeDtypeStruct((24, 1536), F32),
            jax.ShapeDtypeStruct((96, 384), F32),
        ),
        in_specs=[
            whole(81, 96),
            whole(512, 448),
            whole(4, 24, 1152),
            pl.BlockSpec((96, 1, 16, 448), lambda h: (0, h, 0, 0)),
        ],
        out_specs=(
            pl.BlockSpec((96, 1, 16, 448), lambda h: (0, h, 0, 0)),
            whole(128, 128),
            whole(24, 1152),
            whole(24, 384),
            whole(24, 1536),
            whole(96, 384),
        ),
        scratch_shapes=[
            pltpu.VMEM((1536, 432), BF),
            pltpu.VMEM((1296, 512), BF),
            pltpu.VMEM((4, 512, 128), F32),
            pltpu.VMEM((432, 1536), F32),
        ],
        name="conv_backward",
    )(w81, grad_rows, sums, features)


def patch_matrix(patch_weight):
    row = iota((896, 588), 0)
    tile_row = row % 32
    colour, height = tile_row // 9, tile_row % 9
    piece = row // 32
    half, column = piece // 14, piece % 14
    line = (7 * half + height + 13) % 14
    source = colour * 196 + line * 14 + column
    return dot(one_hot((iota((896, 588), 1) == source) & (tile_row < 27)), patch_weight).astype(BF)


def norm_forward(values, gain):
    centered = values - jnp.mean(values, axis=-1, keepdims=True)
    scale = lax.rsqrt(jnp.mean(centered * centered, axis=-1, keepdims=True) + 1e-06)
    unit = centered * scale
    return unit, scale, (unit * gain).astype(BF)


def norm_backward(unit, scale, gain, grad):
    grad = grad * gain
    return scale * (
        grad
        - jnp.mean(grad, axis=-1, keepdims=True)
        - unit * jnp.mean(grad * unit, axis=-1, keepdims=True)
    )


def frame_kernel(
    z_ref, g_ref, pos_ref, pw_ref, n1_ref, wqkv_ref, wproj_ref, n2_ref, w1_ref, w2_ref,
    out_ref, dz_ref, dw_ref,
    wp_ref, a_ref, r_ref, pk_ref, dpk_ref, prob_ref, d2_ref,
):
    wp_ref[...] = patch_matrix(pw_ref[...])
    z = z_ref[...].astype(F32)
    place = iota((512, 448), 0)
    tile, tile_row = place // 32, place % 32
    height = tile_row % 9
    used = tile_row < 27
    above = pltpu.roll(z, 25, 0)
    below = pltpu.roll(z, 487, 0)
    z = z + jnp.where((height == 1) & (tile > 0), above, 0.0)
    z = z + jnp.where((height == 7) & (tile < 15), below, 0.0)
    z = jnp.where(used & (height > 0) & (height < 8), z, 0.0).astype(BF)
    pick = iota((448, 448), 0)
    permute = one_hot(iota((448, 448), 1) == (pick % 32) * 14 + pick // 32)
    turned = dot(permute, z, NT)
    for tile_at in range(16):
        for column in range(14):
            at = ((tile_at % 2) * 14 + column) * 32
            a_ref[tile_at // 2 * 32 : tile_at // 2 * 32 + 32, at : at + 32] = turned[
                column * 32 : column * 32 + 32, tile_at * 32 : tile_at * 32 + 32
            ]
    embedded = dot(a_ref[...].astype(BF), wp_ref[...]) + pos_ref[...].astype(F32)
    gain1, gain2 = n1_ref[...], n2_ref[...]
    unit1, scale1, normed = norm_forward(embedded, gain1)
    pk_ref[...] = dot(normed, wqkv_ref[...]).astype(BF)
    left = iota((256, 128), 1) < 64
    zero = jnp.zeros((256, 128), BF)
    attended = []
    for pair in range(3):
        q = pk_ref[:, pair * 128 : pair * 128 + 128]
        k = pk_ref[:, 384 + pair * 128 : 384 + pair * 128 + 128]
        v = pk_ref[:, 768 + pair * 128 : 768 + pair * 128 + 128]
        both = []
        for side in range(2):
            mine = left if side == 0 else ~left
            s = dot(jnp.where(mine, q, zero), k, NT) * 0.125
            s = jnp.exp(s - jnp.max(s, axis=-1, keepdims=True))
            s = s / jnp.sum(s, axis=-1, keepdims=True)
            prob_ref[pair * 2 + side] = s
            both.append(dot(s.astype(BF), v))
        attended.append(jnp.where(left, both[0], both[1]).astype(BF))
    attended = jnp.concatenate(attended, axis=1)
    residual = embedded + dot(attended, wproj_ref[...])
    unit2, scale2, normed2 = norm_forward(residual, gain2)
    g = g_ref[...]
    out = residual
    dnormed2 = jnp.zeros((256, 384), F32)
    for part in range(2):
        cols = slice(part * 768, part * 768 + 768)
        pre = dot(normed2, w1_ref[:, cols])
        cdf = 0.5 + 0.5 * lax.erf(pre * 0.7071067811865476)
        hidden = (pre * cdf).astype(BF)
        out = out + dot(hidden, w2_ref[cols, :])
        d2 = dot(hidden, g, TN)
        for piece in range(32):
            tile_at, quarter = part * 8 + piece // 4, piece % 4
            d2_ref[quarter, tile_at * 24 : tile_at * 24 + 24, :] = d2[piece * 24 : piece * 24 + 24]
        dhidden = dot(g, w2_ref[cols, :], NT).astype(BF).astype(F32)
        slope = cdf + pre * (0.3989422804014327 * jnp.exp(-0.5 * pre * pre))
        dpre = (dhidden * slope).astype(BF)
        d1 = dot(normed2, dpre, TN).astype(BF)
        dw_ref[1 + part, :, 384 * (1 - part) : 384 * (1 - part) + 768] = d1
        dnormed2 = dnormed2 + dot(dpre, w1_ref[:, cols], NT)
    out_ref[...] = out.astype(BF)
    dw_ref[2, :, 768:] = d2_ref[0].astype(BF)
    for quarter in range(3):
        dw_ref[3, :, quarter * 384 : quarter * 384 + 384] = d2_ref[1 + quarter].astype(BF)
    dnormed2 = dnormed2.astype(BF).astype(F32)
    dres = g.astype(F32) + norm_backward(unit2, scale2, gain2, dnormed2)
    dres_bf = dres.astype(BF)
    dw_ref[1, :, :384] = dot(attended, dres_bf, TN).astype(BF)
    datt = dot(dres_bf, wproj_ref[...], NT).astype(BF)
    for pair in range(3):
        q = pk_ref[:, pair * 128 : pair * 128 + 128]
        k = pk_ref[:, 384 + pair * 128 : 384 + pair * 128 + 128]
        v = pk_ref[:, 768 + pair * 128 : 768 + pair * 128 + 128]
        da = datt[:, pair * 128 : pair * 128 + 128]
        dq, dk, dv = [], [], []
        for side in range(2):
            mine = left if side == 0 else ~left
            p = prob_ref[pair * 2 + side]
            dp = dot(jnp.where(mine, da, zero), v, NT).astype(BF).astype(F32)
            dv.append(dot(p.astype(BF), da, TN))
            ds = p * (dp - jnp.sum(dp * p, axis=-1, keepdims=True)) * 0.125
            ds = ds.astype(BF)
            dq.append(dot(ds, k))
            dk.append(dot(ds, q, TN))
        dpk_ref[:, pair * 128 : pair * 128 + 128] = jnp.where(left, dq[0], dq[1]).astype(BF)
        dpk_ref[:, 384 + pair * 128 : 384 + pair * 128 + 128] = jnp.where(left, dk[0], dk[1]).astype(BF)
        dpk_ref[:, 768 + pair * 128 : 768 + pair * 128 + 128] = jnp.where(left, dv[0], dv[1]).astype(BF)
    dpk = dpk_ref[...]
    dw_ref[0] = dot(normed, dpk, TN).astype(BF)
    dnormed = dot(dpk, wqkv_ref[...], NT).astype(BF).astype(F32)
    demb = dres + norm_backward(unit1, scale1, gain1, dnormed)
    a_ref[...] = dot(demb.astype(BF), wp_ref[...], NT)
    for tile_at in range(16):
        for column in range(14):
            at = ((tile_at % 2) * 14 + column) * 32
            r_ref[column * 32 : column * 32 + 32, tile_at * 32 : tile_at * 32 + 32] = a_ref[
                tile_at // 2 * 32 : tile_at // 2 * 32 + 32, at : at + 32
            ]
    dz = dot(r_ref[...].astype(BF), permute, TN)
    odd = tile % 2 == 1
    nothing = jnp.zeros((64, 448), F32)
    above = jnp.concatenate([nothing, dz[:448]], axis=0)
    below = jnp.concatenate([dz[64:], nothing], axis=0)
    dz = jnp.where((height == 0) & ~odd, above, dz)
    dz = jnp.where((height == 8) & odd, below, dz)
    dz_ref[...] = dz.astype(BF)


def frame_step(z, g, pos, pw, n1, wqkv, wproj, n2, w1, w2):
    return pl.pallas_call(
        frame_kernel,
        out_shape=(
            jax.ShapeDtypeStruct((256, 384), BF),
            jax.ShapeDtypeStruct((512, 448), BF),
            jax.ShapeDtypeStruct((4, 384, 1152), BF),
        ),
        scratch_shapes=[
            pltpu.VMEM((896, 384), BF),
            pltpu.VMEM((256, 896), F32),
            pltpu.VMEM((448, 512), F32),
            pltpu.VMEM((256, 1152), BF),
            pltpu.VMEM((256, 1152), BF),
            pltpu.VMEM((6, 256, 256), F32),
            pltpu.VMEM((4, 384, 384), F32),
        ],
        name="frame_step",
    )(z, g, pos, pw, n1, wqkv, wproj, n2, w1, w2)


def flip(i):
    return i + 1 - 2 * (i % 2)


def across(i):
    return (i + 2) % 4


def mirror(i):
    return 3 - i


class Mailer:
    def __init__(self, send, recv):
        self.send, self.recv, self.count, self.copies = send, recv, 0, []

    def __call__(self, source, target, **where):
        copy = pltpu.make_async_remote_copy(
            src_ref=source,
            dst_ref=target,
            send_sem=self.send.at[self.count],
            recv_sem=self.recv.at[self.count],
            device_id=where,
            device_id_type=pl.DeviceIdType.MESH,
        )
        self.count += 1
        copy.start()
        self.copies.append(copy)
        return copy


def meet(peers):
    barrier = pltpu.get_barrier_semaphore()
    for where in peers:
        pl.semaphore_signal(barrier, inc=1, device_id=where, device_id_type=pl.DeviceIdType.MESH)
    pl.semaphore_wait(barrier, len(peers))


def exchange_kernel(x_ref, o_ref, send, recv, local):
    me = lax.axis_index("space")
    peers = [(me + k) % 16 for k in range(1, 16)]
    own = pltpu.make_async_copy(x_ref.at[me], o_ref.at[me], local)
    own.start()
    meet([{"space": peer} for peer in peers])
    mail = Mailer(send, recv)
    copies = [mail(x_ref.at[peer], o_ref.at[me], space=peer) for peer in peers]
    own.wait()
    for copy in copies:
        copy.wait()


def exchange(rows):
    return pl.pallas_call(
        exchange_kernel,
        out_shape=jax.ShapeDtypeStruct(rows.shape, rows.dtype),
        in_specs=[pl.BlockSpec(memory_space=pl.ANY)],
        out_specs=pl.BlockSpec(memory_space=pl.ANY),
        scratch_shapes=[
            pltpu.SemaphoreType.DMA((15,)),
            pltpu.SemaphoreType.DMA((15,)),
            pltpu.SemaphoreType.DMA,
        ],
        compiler_params=pltpu.CompilerParams(collective_id=0, has_side_effects=True),
        name="exchange",
    )(rows)


def accumulate(target, first, sources):
    count = sources[0].shape[0]

    def body(i, carry):
        total = target[first + i].astype(F32)
        for source in sources:
            total = total + source[i].astype(F32)
        target[first + i] = total.astype(BF)
        return carry

    lax.fori_loop(0, count, body, 0)


def reduce_kernel(
    rows_ref, w_ref, rows_out, sums_ref,
    own, got, z1, z2, y1, y2, x_in, mine, send, recv, local,
):
    space, dp = lax.axis_index("space"), lax.axis_index("dp")
    y, x_hi, core = space // 4, space // 2 % 2, space % 2
    x_lo, z = dp // 4, dp % 4
    peers = [(space + k) % 16 for k in range(1, 16)]

    def at(y_to=y, x_hi_to=x_hi, x_lo_to=x_lo, z_to=z, core_to=core):
        return {"dp": x_lo_to * 4 + z_to, "space": y_to * 4 + x_hi_to * 2 + core_to}

    quarters = [across(z), flip(z), mirror(z), z]
    loads = [pltpu.make_async_copy(w_ref.at[q, :, core], own.at[i], local.at[i]) for i, q in enumerate(quarters)]
    for load in loads:
        load.start()
    own_rows = pltpu.make_async_copy(rows_ref.at[space], rows_out.at[space], local.at[4])
    own_rows.start()
    meet(
        [{"dp": dp, "space": peer} for peer in peers]
        + [at(z_to=flip(z)), at(z_to=mirror(z)), at(z_to=across(z))]
        + [at(x_lo_to=1 - x_lo), at(x_hi_to=1 - x_hi, x_lo_to=1 - x_lo)]
    )
    mail = Mailer(send, recv)
    rows = [mail(rows_ref.at[peer], rows_out.at[space], dp=dp, space=peer) for peer in peers]
    pair = [mail(w_ref.at[q, :, 1 - core], got.at[i], **at(core_to=1 - core)) for i, q in enumerate(quarters)]
    first = []
    for i in range(4):
        loads[i].wait()
        pair[i].wait_recv()
        accumulate(own.at[i], 0, [got.at[i]])
        if i < 2:
            first.append(mail(own.at[i, 0:4], z1.at[i], **at(z_to=flip(z))))
        if i % 2 == 0:
            first.append(mail(own.at[i, 4:8], z1.at[2 + i // 2], **at(z_to=mirror(z))))
    low0, high0, low1, high1 = first
    low0.wait_recv()
    accumulate(own.at[2], 0, [z1.at[0]])
    low2 = mail(own.at[2, 0:4], z2.at[0], **at(z_to=mirror(z)))
    high0.wait_recv()
    accumulate(own.at[1], 4, [z1.at[2]])
    high2 = mail(own.at[1, 4:8], z2.at[1], **at(z_to=flip(z)))
    low1.wait_recv()
    low2.wait_recv()
    accumulate(own.at[3], 0, [z1.at[1], z2.at[0]])
    high1.wait_recv()
    high2.wait_recv()
    accumulate(own.at[3], 4, [z1.at[3], z2.at[1]])
    block = lambda y_of, x_of: own.at[3, pl.ds(y_of * 2 + x_of, 1)]
    low0 = mail(block(across(y), 0), y1.at[0], **at(y_to=flip(y)))
    high0 = mail(block(across(y), 1), y1.at[2], **at(y_to=mirror(y)))
    low1 = mail(block(flip(y), 0), y1.at[1], **at(y_to=flip(y)))
    high1 = mail(block(mirror(y), 1), y1.at[3], **at(y_to=mirror(y)))
    low0.wait_recv()
    accumulate(own.at[3], mirror(y) * 2, [y1.at[0]])
    low2 = mail(block(mirror(y), 0), y2.at[0], **at(y_to=mirror(y)))
    high0.wait_recv()
    accumulate(own.at[3], flip(y) * 2 + 1, [y1.at[2]])
    high2 = mail(block(flip(y), 1), y2.at[1], **at(y_to=flip(y)))
    low1.wait_recv()
    low2.wait_recv()
    accumulate(own.at[3], y * 2, [y1.at[1], y2.at[0]])
    high1.wait_recv()
    high2.wait_recv()
    accumulate(own.at[3], y * 2 + 1, [y1.at[3], y2.at[1]])
    x_mine = x_hi * 2 + x_lo
    lines = [
        mail(own.at[3, y * 2 + hi], x_in.at[x_mine], **at(x_hi_to=hi, x_lo_to=lo))
        for hi, lo in ((1 - x_hi, x_lo), (x_hi, 1 - x_lo), (1 - x_hi, 1 - x_lo))
    ]
    x_in[x_mine] = own[3, y * 2 + x_hi]
    for line in lines:
        line.wait_recv()
    total = x_in[0].astype(F32)
    for i in range(1, 4):
        total = total + x_in[i].astype(F32)
    mine[...] = total.astype(BF)
    sums_ref[z] = total.astype(BF)
    spread = [mail(mine, sums_ref.at[z], **at(z_to=to)) for to in (flip(z), mirror(z), across(z))]
    own_rows.wait()
    for copy in rows + spread:
        copy.wait_recv()
    for copy in mail.copies:
        copy.wait_send()


def reduce_all(rows, weights):
    piece = (24, 1152)
    copies = 37
    return pl.pallas_call(
        reduce_kernel,
        out_shape=(
            jax.ShapeDtypeStruct(rows.shape, BF),
            jax.ShapeDtypeStruct((4, *piece), BF),
        ),
        in_specs=[pl.BlockSpec(memory_space=pl.ANY)] * 2,
        out_specs=(pl.BlockSpec(memory_space=pl.ANY), pl.BlockSpec(memory_space=pltpu.VMEM)),
        scratch_shapes=[
            pltpu.VMEM((4, 8, *piece), BF),
            pltpu.VMEM((4, 8, *piece), BF),
            pltpu.VMEM((4, 4, *piece), BF),
            pltpu.VMEM((2, 4, *piece), BF),
            pltpu.VMEM((4, 1, *piece), BF),
            pltpu.VMEM((2, 1, *piece), BF),
            pltpu.VMEM((4, *piece), BF),
            pltpu.VMEM(piece, BF),
            pltpu.SemaphoreType.DMA((copies,)),
            pltpu.SemaphoreType.DMA((copies,)),
            pltpu.SemaphoreType.DMA((5,)),
        ],
        compiler_params=pltpu.CompilerParams(collective_id=1, has_side_effects=True),
        name="reduce_all",
    )(rows, weights.reshape(4, 8, 2, 24, 1152))


def conv_total_kernel(part_ref, total_ref, by_space, by_dp, send, recv):
    space, dp = lax.axis_index("space"), lax.axis_index("dp")
    across_space = [(space + k) % 16 for k in range(1, 16)]
    across_dp = [(dp + k) % 8 for k in range(1, 8)]
    meet(
        [{"dp": dp, "space": peer} for peer in across_space]
        + [{"dp": peer, "space": space} for peer in across_dp]
    )
    mail = Mailer(send, recv)
    lines = lambda i: pl.ds(pl.multiple_of(i * 8, 8), 8)
    one = [mail(part_ref.at[lines(to)], by_space.at[space], dp=dp, space=to) for to in across_space]
    by_space[space] = part_ref[lines(space), :]
    for copy in one:
        copy.wait_recv()
    total = by_space[0]
    for i in range(1, 16):
        total = total + by_space[i]
    by_dp[dp] = total
    two = [mail(by_dp.at[dp], by_dp.at[dp], dp=to, space=space) for to in across_dp]
    for copy in two:
        copy.wait_recv()
    total = by_dp[0]
    for i in range(1, 8):
        total = total + by_dp[i]
    total_ref[lines(space), :] = total
    three = [mail(total_ref.at[lines(space)], total_ref.at[lines(space)], dp=dp, space=to) for to in across_space]
    for copy in three:
        copy.wait_recv()
    for copy in mail.copies:
        copy.wait_send()


def conv_total(part):
    return pl.pallas_call(
        conv_total_kernel,
        out_shape=jax.ShapeDtypeStruct((128, 128), F32),
        in_specs=[pl.BlockSpec(memory_space=pltpu.VMEM)],
        out_specs=pl.BlockSpec(memory_space=pltpu.VMEM),
        scratch_shapes=[
            pltpu.VMEM((16, 8, 128), F32),
            pltpu.VMEM((8, 8, 128), F32),
            pltpu.SemaphoreType.DMA((37,)),
            pltpu.SemaphoreType.DMA((37,)),
        ],
        compiler_params=pltpu.CompilerParams(collective_id=2, has_side_effects=True),
        name="conv_total",
    )(part)


def shards(
    features, conv_weight, out_grad, pos_embed, patch_weight, norm1, qkv_weight, proj_weight,
    norm2, fc1_weight, fc2_weight,
):
    tile = features[0].transpose(0, 2, 1, 3)
    w81 = conv_weight.reshape(81, 96)
    rows = exchange(conv_forward(tile, w81).reshape(16, 32, 448))
    block_out, grad_rows, weights = frame_step(
        rows.reshape(512, 448), out_grad[0, 0], pos_embed, patch_weight, norm1[None],
        qkv_weight, proj_weight, norm2[None], fc1_weight, fc2_weight,
    )
    grad_rows, sums = reduce_all(grad_rows.reshape(16, 32, 448), weights)
    feature_grad, conv_part, *shares = conv_backward(tile, w81, grad_rows.reshape(512, 448), sums)
    conv_sum = conv_total(conv_part)
    return (
        block_out[None, None],
        feature_grad.transpose(0, 2, 1, 3)[None],
        conv_sum[:81, :96].reshape(conv_weight.shape),
        *shares,
    )


def solution(mesh):
    placed = (
        P("dp", None, None, "space", None),
        P(),
        P("dp", "space", None, None),
        *([P()] * 8),
    )
    return jax.shard_map(
        shards,
        mesh=mesh,
        in_specs=placed,
        out_specs=(
            P("dp", "space", None, None),
            P("dp", None, None, "space", None),
            P(),
            *([P("space", None)] * 4),
        ),
        check_vma=False,
    )
```

```python
import functools

import jax
import jax.numpy as jnp
from jax import lax
from jax.experimental import pallas as pl
from jax.experimental.pallas import tpu as pltpu
from jax.sharding import PartitionSpec as P

HEADS = 6
BF = jnp.bfloat16
F32 = jnp.float32
NN = (((1,), (0,)), ((), ()))
NT = (((1,), (1,)), ((), ()))
TN = (((0,), (0,)), ((), ()))


def dot(a, b, dims=NN):
    return lax.dot_general(a, b, dims, preferred_element_type=F32)


def iota(shape, dim):
    return lax.broadcasted_iota(jnp.int32, shape, dim)


def one_hot(cond):
    return jnp.where(cond, 1.0, 0.0).astype(BF)


def tap_rows(w, a):
    rows = [
        jnp.broadcast_to(w[a, 2 - b, e, o : o + 1, :], (16, 96))
        for b in range(3)
        for e in range(3)
        for o in range(3)
    ]
    return jnp.concatenate(rows, axis=0).astype(BF)


def band(w):
    spread = one_hot(iota((96, 1536), 1) // 16 == iota((96, 1536), 0))
    lag = iota((432, 1536), 1) % 16 - iota((432, 1536), 0) % 16 + 2
    total = None
    for a in range(3):
        piece = jnp.where(lag == a, dot(tap_rows(w, a), spread), 0.0)
        total = piece if total is None else total + piece
    return total.astype(BF)


def band_transposed(w):
    spread = one_hot(iota((1536, 96), 0) // 16 == iota((1536, 96), 1))
    lag = iota((1536, 432), 0) % 16 - iota((1536, 432), 1) % 16 + 2
    total = None
    for a in range(3):
        piece = jnp.where(lag == a, dot(spread, tap_rows(w, a), NT), 0.0)
        total = piece if total is None else total + piece
    return total.astype(BF)


def batch_place(row, colour):
    return (row // 5, (row % 5) * 3 + colour)


def conv_forward_kernel(w_ref, x_ref, out_ref, band_ref, acc_ref, rows_ref, post, send, recv, local):
    step = pl.program_id(0)
    me = lax.axis_index("space")
    peers = [(me + k) % 16 for k in range(1, 16)]

    @pl.when(step == 0)
    def _():
        barrier = pltpu.get_barrier_semaphore()
        for peer in peers:
            pl.semaphore_signal(
                barrier, inc=1, device_id={"space": peer}, device_id_type=pl.DeviceIdType.MESH
            )
        band_ref[...] = band(w_ref[...].astype(F32))
        acc_ref[...] = jnp.zeros_like(acc_ref)
        rows_ref[...] = jnp.zeros_like(rows_ref)

    x = x_ref[:, 0].reshape(1536, 448)
    at = pl.ds(pl.multiple_of(step * 144, 16), 432)
    acc_ref[at, :448] += dot(band_ref[...], x)

    def copies(batch):
        return [
            pltpu.make_async_remote_copy(
                src_ref=post.at[batch, peer],
                dst_ref=out_ref.at[batch, me],
                send_sem=send.at[batch * 15 + i],
                recv_sem=recv.at[batch * 15 + i],
                device_id={"space": peer},
                device_id_type=pl.DeviceIdType.MESH,
            )
            for i, peer in enumerate(peers)
        ]

    def mail(batch):
        for row in range(5) if batch == 0 else range(5, 9):
            taps = acc_ref[row * 144 : (row + 1) * 144, :]
            out = pltpu.roll(taps[0:48], 1, 1) + taps[48:96] + pltpu.roll(taps[96:144], 511, 1)
            for o in range(3):
                for t in range(4):
                    rows_ref[t, pl.ds(batch_place(row, o)[1], 16, stride=16), :] = out[
                        o * 16 : (o + 1) * 16, t * 128 : t * 128 + 128
                    ]
        for t in range(3):
            post[batch, :, :, t * 128 : t * 128 + 128] = rows_ref[t].reshape(16, 16, 128).astype(BF)
        post[batch, :, :, 384:448] = rows_ref[3, :, :64].reshape(16, 16, 64).astype(BF)
        for copy in copies(batch):
            copy.start()
        pltpu.make_async_copy(post.at[batch, me], out_ref.at[batch, me], local.at[batch]).start()

    @pl.when(step == 4)
    def _():
        pl.semaphore_wait(pltpu.get_barrier_semaphore(), 15)
        mail(0)

    @pl.when(step == 6)
    def _():
        mail(1)
        for batch in range(2):
            pltpu.make_async_copy(post.at[batch, me], out_ref.at[batch, me], local.at[batch]).wait()
            for copy in copies(batch):
                copy.wait()


def conv_forward(features, conv_weight):
    return pl.pallas_call(
        conv_forward_kernel,
        grid=(7,),
        out_shape=jax.ShapeDtypeStruct((2, 16, 16, 448), BF),
        in_specs=[
            pl.BlockSpec((3, 3, 3, 3, 96), lambda h: (0, 0, 0, 0, 0)),
            pl.BlockSpec((96, 1, 16, 448), lambda h: (0, h, 0, 0)),
        ],
        out_specs=pl.BlockSpec(memory_space=pl.ANY),
        scratch_shapes=[
            pltpu.VMEM((432, 1536), BF),
            pltpu.VMEM((1296, 512), F32),
            pltpu.VMEM((4, 256, 128), F32),
            pltpu.VMEM((2, 16, 16, 448), BF),
            pltpu.SemaphoreType.DMA((30,)),
            pltpu.SemaphoreType.DMA((30,)),
            pltpu.SemaphoreType.DMA((2,)),
        ],
        compiler_params=pltpu.CompilerParams(collective_id=0, has_side_effects=True),
        name="conv_forward",
    )(conv_weight, features)


def feature_gradient_kernel(band_ref, pg_ref, sums_ref, fg_ref, qkv_ref, proj_ref, fc1_ref, fc2_ref):
    step = pl.program_id(0)

    @pl.when(step == 1)
    def _():
        qkv_ref[...] = sums_ref[0].astype(F32)
        proj_ref[...] = sums_ref[1, :, :384].astype(F32)
        fc1_ref[:, :768] = sums_ref[1, :, 384:].astype(F32)
        fc1_ref[:, 768:] = sums_ref[2, :, :768].astype(F32)
        fc2_ref[0:24] = sums_ref[2, :, 768:].astype(F32)
        for quarter in range(3):
            at = quarter * 24 + 24
            fc2_ref[at : at + 24] = sums_ref[3, :, quarter * 384 : quarter * 384 + 384].astype(F32)

    pg = pg_ref[pl.ds(pl.multiple_of(step * 144, 16), 432), :448]
    fg_ref[:, 0] = dot(band_ref[...], pg).astype(BF).reshape(96, 16, 448)


def feature_gradient(back, pixel_taps, sums):
    whole = lambda *shape: pl.BlockSpec(shape, lambda h: (0,) * len(shape))
    return pl.pallas_call(
        feature_gradient_kernel,
        grid=(7,),
        out_shape=(
            jax.ShapeDtypeStruct((96, 7, 16, 448), BF),
            jax.ShapeDtypeStruct((24, 1152), F32),
            jax.ShapeDtypeStruct((24, 384), F32),
            jax.ShapeDtypeStruct((24, 1536), F32),
            jax.ShapeDtypeStruct((96, 384), F32),
        ),
        in_specs=[whole(1536, 432), whole(1296, 512), whole(4, 24, 1152)],
        out_specs=(
            pl.BlockSpec((96, 1, 16, 448), lambda h: (0, h, 0, 0)),
            whole(24, 1152),
            whole(24, 384),
            whole(24, 1536),
            whole(96, 384),
        ),
        name="feature_gradient",
    )(back, pixel_taps, sums)


def patch_matrix(patch_weight):
    row = iota((896, 588), 0)
    tile_row = row % 32
    place = tile_row - tile_row // 16
    colour, height = place % 3, place // 3
    piece = row // 32
    half, column = piece // 14, piece % 14
    line = (7 * half + height + 13) % 14
    source = colour * 196 + line * 14 + column
    return dot(one_hot((iota((896, 588), 1) == source) & (tile_row < 28) & (tile_row != 15)), patch_weight).astype(BF)


def norm_forward(values, gain):
    centered = values - jnp.mean(values, axis=-1, keepdims=True)
    scale = lax.rsqrt(jnp.mean(centered * centered, axis=-1, keepdims=True) + 1e-06)
    unit = centered * scale
    return unit, scale, (unit * gain).astype(BF)


def norm_backward(unit, scale, gain, grad):
    grad = grad * gain
    return scale * (
        grad
        - jnp.mean(grad, axis=-1, keepdims=True)
        - unit * jnp.mean(grad * unit, axis=-1, keepdims=True)
    )


def frame_kernel(
    z_ref, g_ref, pos_ref, pw_ref, n1_ref, wqkv_ref, wproj_ref, n2_ref, w1_ref, w2_ref,
    out_ref, dz_ref, dw_ref,
    wp_ref, a_ref, r_ref, pk_ref, dpk_ref, prob_ref, d2_ref,
):
    wp_ref[...] = patch_matrix(pw_ref[...])
    z = jnp.concatenate([z_ref[0].astype(F32), z_ref[1].astype(F32)], axis=1).reshape(512, 448)
    place = iota((512, 448), 0)
    tile, tile_row = place // 32, place % 32
    height = (tile_row - tile_row // 16) // 3
    used = (tile_row < 28) & (tile_row != 15)
    above = pltpu.roll(z, 10, 0)
    below = pltpu.roll(z, 502, 0)
    z = z + jnp.where((height == 1) & (tile > 0), above, 0.0)
    z = z + jnp.where((height == 7) & (tile < 15), below, 0.0)
    z = jnp.where(used & (height > 0) & (height < 8), z, 0.0).astype(BF)
    pick = iota((448, 448), 0)
    permute = one_hot(iota((448, 448), 1) == (pick % 32) * 14 + pick // 32)
    turned = dot(permute, z, NT)
    for tile_at in range(16):
        for column in range(14):
            at = ((tile_at % 2) * 14 + column) * 32
            a_ref[tile_at // 2 * 32 : tile_at // 2 * 32 + 32, at : at + 32] = turned[
                column * 32 : column * 32 + 32, tile_at * 32 : tile_at * 32 + 32
            ]
    embedded = dot(a_ref[...].astype(BF), wp_ref[...]) + pos_ref[...].astype(F32)
    gain1, gain2 = n1_ref[...].reshape(1, 384), n2_ref[...].reshape(1, 384)
    unit1, scale1, normed = norm_forward(embedded, gain1)
    pk_ref[...] = dot(normed, wqkv_ref[...]).astype(BF)
    left = iota((256, 128), 1) < 64
    zero = jnp.zeros((256, 128), BF)
    attended = []
    for pair in range(3):
        q = pk_ref[:, pair * 128 : pair * 128 + 128]
        k = pk_ref[:, 384 + pair * 128 : 384 + pair * 128 + 128]
        v = pk_ref[:, 768 + pair * 128 : 768 + pair * 128 + 128]
        both = []
        for side in range(2):
            mine = left if side == 0 else ~left
            s = dot(jnp.where(mine, q, zero), k, NT) * 0.125
            s = jnp.exp(s - jnp.max(s, axis=-1, keepdims=True))
            s = s / jnp.sum(s, axis=-1, keepdims=True)
            prob_ref[pair * 2 + side] = s
            both.append(dot(s.astype(BF), v))
        attended.append(jnp.where(left, both[0], both[1]).astype(BF))
    attended = jnp.concatenate(attended, axis=1)
    residual = embedded + dot(attended, wproj_ref[...])
    unit2, scale2, normed2 = norm_forward(residual, gain2)
    g = g_ref[...]
    out = residual
    dnormed2 = jnp.zeros((256, 384), F32)
    for part in range(2):
        cols = slice(part * 768, part * 768 + 768)
        pre = dot(normed2, w1_ref[:, cols])
        cdf = 0.5 + 0.5 * lax.erf(pre * 0.7071067811865476)
        hidden = (pre * cdf).astype(BF)
        out = out + dot(hidden, w2_ref[cols, :])
        d2 = dot(hidden, g, TN)
        for piece in range(32):
            tile_at, quarter = part * 8 + piece // 4, piece % 4
            d2_ref[quarter, tile_at * 24 : tile_at * 24 + 24, :] = d2[piece * 24 : piece * 24 + 24]
        dhidden = dot(g, w2_ref[cols, :], NT).astype(BF).astype(F32)
        slope = cdf + pre * (0.3989422804014327 * jnp.exp(-0.5 * pre * pre))
        dpre = (dhidden * slope).astype(BF)
        d1 = dot(normed2, dpre, TN).astype(BF)
        dw_ref[1 + part, :, 384 * (1 - part) : 384 * (1 - part) + 768] = d1
        dnormed2 = dnormed2 + dot(dpre, w1_ref[:, cols], NT)
    out_ref[...] = out.astype(BF)
    dw_ref[2, :, 768:] = d2_ref[0].astype(BF)
    for quarter in range(3):
        dw_ref[3, :, quarter * 384 : quarter * 384 + 384] = d2_ref[1 + quarter].astype(BF)
    dnormed2 = dnormed2.astype(BF).astype(F32)
    dres = g.astype(F32) + norm_backward(unit2, scale2, gain2, dnormed2)
    dres_bf = dres.astype(BF)
    dw_ref[1, :, :384] = dot(attended, dres_bf, TN).astype(BF)
    datt = dot(dres_bf, wproj_ref[...], NT).astype(BF)
    for pair in range(3):
        q = pk_ref[:, pair * 128 : pair * 128 + 128]
        k = pk_ref[:, 384 + pair * 128 : 384 + pair * 128 + 128]
        v = pk_ref[:, 768 + pair * 128 : 768 + pair * 128 + 128]
        da = datt[:, pair * 128 : pair * 128 + 128]
        dq, dk, dv = [], [], []
        for side in range(2):
            mine = left if side == 0 else ~left
            p = prob_ref[pair * 2 + side]
            dp = dot(jnp.where(mine, da, zero), v, NT).astype(BF).astype(F32)
            dv.append(dot(p.astype(BF), da, TN))
            ds = p * (dp - jnp.sum(dp * p, axis=-1, keepdims=True)) * 0.125
            ds = ds.astype(BF)
            dq.append(dot(ds, k))
            dk.append(dot(ds, q, TN))
        dpk_ref[:, pair * 128 : pair * 128 + 128] = jnp.where(left, dq[0], dq[1]).astype(BF)
        dpk_ref[:, 384 + pair * 128 : 384 + pair * 128 + 128] = jnp.where(left, dk[0], dk[1]).astype(BF)
        dpk_ref[:, 768 + pair * 128 : 768 + pair * 128 + 128] = jnp.where(left, dv[0], dv[1]).astype(BF)
    dpk = dpk_ref[...]
    dw_ref[0] = dot(normed, dpk, TN).astype(BF)
    dnormed = dot(dpk, wqkv_ref[...], NT).astype(BF).astype(F32)
    demb = dres + norm_backward(unit1, scale1, gain1, dnormed)
    a_ref[...] = dot(demb.astype(BF), wp_ref[...], NT)
    for tile_at in range(16):
        for column in range(14):
            at = ((tile_at % 2) * 14 + column) * 32
            r_ref[column * 32 : column * 32 + 32, tile_at * 32 : tile_at * 32 + 32] = a_ref[
                tile_at // 2 * 32 : tile_at // 2 * 32 + 32, at : at + 32
            ]
    dz = dot(r_ref[...].astype(BF), permute, TN)
    odd = tile % 2 == 1
    nothing = jnp.zeros((64, 448), F32)
    above = jnp.concatenate([nothing, dz[:448]], axis=0)
    below = jnp.concatenate([dz[64:], nothing], axis=0)
    dz = jnp.where((height == 0) & ~odd, above, dz)
    dz = jnp.where((height == 8) & odd, below, dz)
    dz = dz.reshape(16, 32, 448)
    dz_ref[0] = dz[:, :16].astype(BF)
    dz_ref[1] = dz[:, 16:].astype(BF)


def frame_step(z, g, pos, pw, n1, wqkv, wproj, n2, w1, w2):
    return pl.pallas_call(
        frame_kernel,
        out_shape=(
            jax.ShapeDtypeStruct((256, 384), BF),
            jax.ShapeDtypeStruct((2, 16, 16, 448), BF),
            jax.ShapeDtypeStruct((4, 384, 1152), BF),
        ),
        scratch_shapes=[
            pltpu.VMEM((896, 384), BF),
            pltpu.VMEM((256, 896), F32),
            pltpu.VMEM((448, 512), F32),
            pltpu.VMEM((256, 1152), BF),
            pltpu.VMEM((256, 1152), BF),
            pltpu.VMEM((6, 256, 256), F32),
            pltpu.VMEM((4, 384, 384), F32),
        ],
        name="frame_step",
    )(z, g, pos, pw, n1, wqkv, wproj, n2, w1, w2)


def flip(i):
    return i + 1 - 2 * (i % 2)


def across(i):
    return (i + 2) % 4


def mirror(i):
    return 3 - i


class Mailer:
    def __init__(self, send, recv):
        self.send, self.recv, self.count, self.copies = send, recv, 0, []

    def __call__(self, source, target, **where):
        copy = pltpu.make_async_remote_copy(
            src_ref=source,
            dst_ref=target,
            send_sem=self.send.at[self.count],
            recv_sem=self.recv.at[self.count],
            device_id=where,
            device_id_type=pl.DeviceIdType.MESH,
        )
        self.count += 1
        copy.start()
        self.copies.append(copy)
        return copy


def meet(peers):
    barrier = pltpu.get_barrier_semaphore()
    for where in peers:
        pl.semaphore_signal(barrier, inc=1, device_id=where, device_id_type=pl.DeviceIdType.MESH)
    pl.semaphore_wait(barrier, len(peers))


def accumulate(target, first, sources):
    count = sources[0].shape[0]

    def body(i, carry):
        total = target[first + i].astype(F32)
        for source in sources:
            total = total + source[i].astype(F32)
        target[first + i] = total.astype(BF)
        return carry

    lax.fori_loop(0, count, body, 0)


def reduce_kernel(
    rows_ref, w_ref, x_ref, cw_ref, sums_ref, conv_ref, pg_ref, back_ref,
    own, got, z1, z2, y1, y2, x_in, mine,
    x, rows_in, rows_f32, g_ref, part, by_space, by_dp,
    send, recv, local,
):
    space, dp = lax.axis_index("space"), lax.axis_index("dp")
    y, x_hi, core = space // 4, space // 2 % 2, space % 2
    x_lo, z = dp // 4, dp % 4
    peers = [(space + k) % 16 for k in range(1, 16)]
    dp_peers = [(dp + k) % 8 for k in range(1, 8)]

    def at(y_to=y, x_hi_to=x_hi, x_lo_to=x_lo, z_to=z, core_to=core):
        return {"dp": x_lo_to * 4 + z_to, "space": y_to * 4 + x_hi_to * 2 + core_to}

    quarters = [across(z), flip(z), mirror(z), z]
    loads = [pltpu.make_async_copy(w_ref.at[q, :, core], own.at[i], local.at[i]) for i, q in enumerate(quarters)]
    own_rows = pltpu.make_async_copy(rows_ref.at[:, space], rows_in.at[:, space], local.at[4])
    features = [pltpu.make_async_copy(x_ref.at[:, h], x.at[h], local.at[5 + h]) for h in range(7)]
    for load in loads + [own_rows] + features:
        load.start()
    meet(
        [{"dp": dp, "space": peer} for peer in peers]
        + [{"dp": peer, "space": space} for peer in dp_peers]
        + [at(x_hi_to=1 - x_hi, x_lo_to=1 - x_lo)]
    )
    mail = Mailer(send, recv)
    rows = [mail(rows_ref.at[:, peer], rows_in.at[:, space], dp=dp, space=peer) for peer in peers]
    pair = [mail(w_ref.at[q, :, 1 - core], got.at[i], **at(core_to=1 - core)) for i, q in enumerate(quarters)]
    first = []
    for i in range(4):
        loads[i].wait()
        pair[i].wait_recv()
        accumulate(own.at[i], 0, [got.at[i]])
        if i < 2:
            first.append(mail(own.at[i, 0:4], z1.at[i], **at(z_to=flip(z))))
        if i % 2 == 0:
            first.append(mail(own.at[i, 4:8], z1.at[2 + i // 2], **at(z_to=mirror(z))))
    own_rows.wait()
    for copy in rows:
        copy.wait_recv()
    rows_f32[3] = jnp.zeros((512, 128), F32)
    for batch in range(2):
        half = slice(batch * 256, batch * 256 + 256)
        for t in range(3):
            rows_f32[t, half] = rows_in[batch, :, :, t * 128 : t * 128 + 128].astype(F32).reshape(256, 128)
        rows_f32[3, half, :64] = rows_in[batch, :, :, 384:448].astype(F32).reshape(256, 64)
    for row in range(9):
        for o in range(3):
            batch, place = batch_place(row, o)
            v = jnp.concatenate(
                [rows_f32[t, pl.ds(batch * 256 + place, 16, stride=16), :] for t in range(4)], axis=1
            )
            for e in range(3):
                moved = v if e == 1 else pltpu.roll(v, 511 if e == 0 else 1, 1)
                to = (row * 9 + e * 3 + o) * 16
                pg_ref[to : to + 16, :] = moved.astype(BF)
    g_ref[...] = jnp.zeros_like(g_ref)

    def conv_rows(start, stop):
        for h in range(start, stop):
            features[h].wait()

        def body(h, carry):
            taps = pg_ref[pl.ds(pl.multiple_of(h * 144, 16), 432), :448]
            g_ref[...] += dot(taps, x[h].reshape(1536, 448), NT)
            return carry

        lax.fori_loop(start, stop, body, 0)

    conv_rows(0, 3)
    low0, high0, low1, high1 = first
    low0.wait_recv()
    accumulate(own.at[2], 0, [z1.at[0]])
    low2 = mail(own.at[2, 0:4], z2.at[0], **at(z_to=mirror(z)))
    high0.wait_recv()
    accumulate(own.at[1], 4, [z1.at[2]])
    high2 = mail(own.at[1, 4:8], z2.at[1], **at(z_to=flip(z)))
    conv_rows(3, 7)
    part[...] = jnp.zeros_like(part)
    spread = one_hot(iota((1536, 96), 0) // 16 == iota((1536, 96), 1))
    lag = iota((16, 1536), 1) % 16 - iota((16, 1536), 0) + 2
    for a in range(3):
        keep = lag == a
        sums = [
            jnp.sum(jnp.where(keep, g_ref[g * 16 : (g + 1) * 16, :], 0.0), axis=0, keepdims=True)
            for g in range(27)
        ]
        sums = [sums[(2 - b) * 9 + eo] for b in range(3) for eo in range(9)]
        total = jnp.concatenate(sums, axis=0)
        high = total.astype(BF)
        rest = (total - high.astype(F32)).astype(BF)
        part[a * 27 : (a + 1) * 27, :96] = dot(high, spread) + dot(rest, spread)
    lines = lambda i: pl.ds(pl.multiple_of(i * 8, 8), 8)
    conv_one = [mail(part.at[lines(to)], by_space.at[space], dp=dp, space=to) for to in peers]
    by_space[space] = part[lines(space), :]
    low1.wait_recv()
    low2.wait_recv()
    accumulate(own.at[3], 0, [z1.at[1], z2.at[0]])
    high1.wait_recv()
    high2.wait_recv()
    accumulate(own.at[3], 4, [z1.at[3], z2.at[1]])
    block = lambda y_of, x_of: own.at[3, pl.ds(y_of * 2 + x_of, 1)]
    low0 = mail(block(across(y), 0), y1.at[0], **at(y_to=flip(y)))
    high0 = mail(block(across(y), 1), y1.at[2], **at(y_to=mirror(y)))
    low1 = mail(block(flip(y), 0), y1.at[1], **at(y_to=flip(y)))
    high1 = mail(block(mirror(y), 1), y1.at[3], **at(y_to=mirror(y)))
    for copy in conv_one:
        copy.wait_recv()
    total = by_space[0]
    for i in range(1, 16):
        total = total + by_space[i]
    by_dp[dp] = total
    conv_two = [mail(by_dp.at[dp], by_dp.at[dp], dp=to, space=space) for to in dp_peers]
    low0.wait_recv()
    accumulate(own.at[3], mirror(y) * 2, [y1.at[0]])
    low2 = mail(block(mirror(y), 0), y2.at[0], **at(y_to=mirror(y)))
    high0.wait_recv()
    accumulate(own.at[3], flip(y) * 2 + 1, [y1.at[2]])
    high2 = mail(block(flip(y), 1), y2.at[1], **at(y_to=flip(y)))
    back_ref[...] = band_transposed(cw_ref[...].astype(F32))
    for copy in conv_two:
        copy.wait_recv()
    total = by_dp[0]
    for i in range(1, 8):
        total = total + by_dp[i]
    conv_ref[lines(space), :] = total
    conv_three = [mail(conv_ref.at[lines(space)], conv_ref.at[lines(space)], dp=dp, space=to) for to in peers]
    low1.wait_recv()
    low2.wait_recv()
    accumulate(own.at[3], y * 2, [y1.at[1], y2.at[0]])
    high1.wait_recv()
    high2.wait_recv()
    accumulate(own.at[3], y * 2 + 1, [y1.at[3], y2.at[1]])
    x_mine = x_hi * 2 + x_lo
    along_x = [
        mail(own.at[3, y * 2 + hi], x_in.at[x_mine], **at(x_hi_to=hi, x_lo_to=lo))
        for hi, lo in ((1 - x_hi, x_lo), (x_hi, 1 - x_lo), (1 - x_hi, 1 - x_lo))
    ]
    x_in[x_mine] = own[3, y * 2 + x_hi]
    for copy in along_x:
        copy.wait_recv()
    total = x_in[0].astype(F32)
    for i in range(1, 4):
        total = total + x_in[i].astype(F32)
    mine[...] = total.astype(BF)
    sums_ref[z] = total.astype(BF)
    final = [mail(mine, sums_ref.at[z], **at(z_to=to)) for to in (flip(z), mirror(z), across(z))]
    for copy in conv_three + final:
        copy.wait_recv()
    for copy in mail.copies:
        copy.wait_send()


def reduce_all(rows, weights, features, conv_weight):
    piece = (24, 1152)
    copies = 37 + 37
    vmem = pl.BlockSpec(memory_space=pltpu.VMEM)
    hbm = pl.BlockSpec(memory_space=pl.ANY)
    return pl.pallas_call(
        reduce_kernel,
        out_shape=(
            jax.ShapeDtypeStruct((4, *piece), BF),
            jax.ShapeDtypeStruct((128, 128), F32),
            jax.ShapeDtypeStruct((1296, 512), BF),
            jax.ShapeDtypeStruct((1536, 432), BF),
        ),
        in_specs=[hbm, hbm, hbm, vmem],
        out_specs=(vmem, vmem, vmem, vmem),
        scratch_shapes=[
            pltpu.VMEM((4, 8, *piece), BF),
            pltpu.VMEM((4, 8, *piece), BF),
            pltpu.VMEM((4, 4, *piece), BF),
            pltpu.VMEM((2, 4, *piece), BF),
            pltpu.VMEM((4, 1, *piece), BF),
            pltpu.VMEM((2, 1, *piece), BF),
            pltpu.VMEM((4, *piece), BF),
            pltpu.VMEM(piece, BF),
            pltpu.VMEM((7, 96, 16, 448), BF),
            pltpu.VMEM((2, 16, 16, 448), BF),
            pltpu.VMEM((4, 512, 128), F32),
            pltpu.VMEM((432, 1536), F32),
            pltpu.VMEM((128, 128), F32),
            pltpu.VMEM((16, 8, 128), F32),
            pltpu.VMEM((8, 8, 128), F32),
            pltpu.SemaphoreType.DMA((copies,)),
            pltpu.SemaphoreType.DMA((copies,)),
            pltpu.SemaphoreType.DMA((12,)),
        ],
        compiler_params=pltpu.CompilerParams(collective_id=1, has_side_effects=True),
        name="reduce_all",
    )(rows, weights.reshape(4, 8, 2, 24, 1152), features, conv_weight)


def shards(
    features, conv_weight, out_grad, pos_embed, patch_weight, norm1, qkv_weight, proj_weight,
    norm2, fc1_weight, fc2_weight,
):
    tile = features[0].transpose(0, 2, 1, 3)
    block_out, grad_rows, weights = frame_step(
        conv_forward(tile, conv_weight), out_grad[0, 0], pos_embed, patch_weight, norm1,
        qkv_weight, proj_weight, norm2, fc1_weight, fc2_weight,
    )
    sums, conv_sum, pixel_taps, back = reduce_all(grad_rows, weights, tile, conv_weight)
    feature_grad, *shares = feature_gradient(back, pixel_taps, sums)
    return (
        block_out[None, None],
        feature_grad.transpose(0, 2, 1, 3)[None],
        conv_sum[:81, :96].reshape(conv_weight.shape),
        *shares,
    )


def solution(mesh):
    placed = (
        P("dp", None, None, "space", None),
        P(),
        P("dp", "space", None, None),
        *([P()] * 8),
    )
    return jax.shard_map(
        shards,
        mesh=mesh,
        in_specs=placed,
        out_specs=(
            P("dp", "space", None, None),
            P("dp", None, None, "space", None),
            P(),
            *([P("space", None)] * 4),
        ),
        check_vma=False,
    )
```
